32 devices in a mesh: tm: 8 (over z, core), space: 4 (over y, x).
Axes of the slice: x: 2, y: 2, z: 4, core: 2. Of those that a mesh axis runs over, the one named last changes fastest.
Arguments:
- start_state: float32 [3, 32, 2048], P(None, 'space'), may hold values from -2 to 2
- still_depth: float32 [32, 2048], P('space'), may hold values from 0.25 to 1
- coriolis: float32 [32, 2048], P('space'), may hold values from -0.3 to 0.3
- drag_rate: float32 [32, 2048], P('space'), may hold values from 0.002 to 0.3
Outputs:
- slice_ends: float32 [8, 3, 32, 2048], P('tm', None, 'space')
The draws below stay inside these ranges and needn't reach their ends.
All inputs are finite; a program needn't handle non-finite values.
Results may differ from the reference program's by a relative error of at most 0.00002.
Values sent between devices are 32-bit elements; how exact they have to be, the bound alone decides.
A program may use at most 64 MiB of HBM per device.

```python
import math
import jax
import jax.numpy as jnp
from jax import lax

NY = 2048
FINE = 4
ITERS = 2
NX = 32
N_TM = 8


def block_scale(rng, dims, cuts, least, high):
    level, own = 1.0, jax.random.fold_in(rng, 6)
    for position, shards_of in cuts:
        heights = jnp.exp(jax.random.uniform(jax.random.fold_in(own, position), (shards_of,), jnp.float32, least / len(cuts), high / len(cuts)))
        level = level * jnp.repeat(heights, dims[position] // shards_of).reshape([-1 if axis == position else 1 for axis in range(len(dims))])
    return level


def noise(stream_key, shape, scale, limit, shards=(), kind=jnp.bfloat16):
    factor_of = block_scale(stream_key, shape, shards, -0.22, 0.18) if shards else 1.0
    entries = jax.random.normal(stream_key, shape, jnp.float32) * scale * factor_of
    return jnp.minimum(jnp.maximum(entries, -limit), limit).astype(kind)


def setup_inputs(seed: int = 0) -> dict:
    splits = jax.random.split(jax.random.key(seed), 5)
    start_state = noise(splits[0], (3, NX, NY), 0.3, 2.0, ((1, 4),), jnp.float32)
    still_depth = jnp.clip(0.25 + 0.75 * jax.random.uniform(splits[1], (NX, NY), jnp.float32) ** block_scale(splits[1], (NX, NY), ((0, 4),), -0.2, 0.2), 0.25, 1.0)
    coriolis = jnp.clip(jax.random.uniform(splits[2], (NX, NY), jnp.float32, -0.3, 0.3) * block_scale(splits[2], (NX, NY), ((0, 4),), -0.4, 0.0), -0.3, 0.3)
    drag_rate = jnp.clip(jnp.exp(math.log(0.3) - 5.0106353 * jax.random.uniform(splits[3], (NX, NY), jnp.float32) ** block_scale(splits[3], (NX, NY), ((0, 4),), -0.2, 0.2)), 0.002, 0.3)
    return {"start_state": start_state, "still_depth": still_depth, "coriolis": coriolis, "drag_rate": drag_rate}


step_len = 1.3


def coarse_power(steps_done, decay_total, turn_angle):
    damping = jnp.exp(-steps_done * decay_total)
    return damping * jnp.cos(steps_done * turn_angle), -damping * jnp.sin(steps_done * turn_angle)


def rotate(fields, part_re, part_im):
    height = fields[..., 0, :, :]
    along_x = fields[..., 1, :, :]
    along_y = fields[..., 2, :, :]
    turned_x = part_re * along_x - part_im * along_y
    turned_y = part_im * along_x + part_re * along_y
    return jnp.stack([jnp.broadcast_to(height, turned_x.shape), turned_x, turned_y], axis=-3)


def fine_step(fields, still_depth, cosine, sine_step, damping):
    height = fields[0]
    along_x = fields[1]
    along_y = fields[2]
    flux_x = still_depth * along_x
    flux_y = still_depth * along_y
    divergence = (jnp.roll(flux_x, -1, 0) - jnp.roll(flux_x, 1, 0)) * 0.5 + (jnp.roll(flux_y, -1, 1) - jnp.roll(flux_y, 1, 1)) * 0.5
    height_new = height - step_len * divergence
    slope_x = (jnp.roll(height_new, -1, 0) - jnp.roll(height_new, 1, 0)) * 0.5
    slope_y = (jnp.roll(height_new, -1, 1) - jnp.roll(height_new, 1, 1)) * 0.5
    new_x = damping * (cosine * along_x + sine_step * along_y) - step_len * slope_x
    new_y = damping * (cosine * along_y - sine_step * along_x) - step_len * slope_y
    return jnp.stack([height_new, new_x, new_y])


def reference(start_state, still_depth, coriolis, drag_rate):
    turn_angle = FINE * step_len * coriolis
    decay_total = FINE * drag_rate
    cosine = jnp.cos(step_len * coriolis)
    sine_step = jnp.sin(step_len * coriolis)
    damping = jnp.exp(-drag_rate)
    slice_ids = jnp.arange(N_TM, dtype=jnp.float32)[:, None, None]
    power_re, power_im = coarse_power(slice_ids, decay_total, turn_angle)
    starts = rotate(start_state[None], power_re, power_im)
    coarse_re, coarse_im = coarse_power(1.0, decay_total, turn_angle)

    def propagate(fields):
        for repeat in range(FINE):
            fields = fine_step(fields, still_depth, cosine, sine_step, damping)
        return fields

    def sweep(carry, jump_one):
        nexted = rotate(carry, coarse_re, coarse_im) + jump_one
        return nexted, (carry, nexted)

    slice_ends = starts
    for repeat in range(ITERS):
        fine_end = lax.map(propagate, starts)
        jump_terms = fine_end - rotate(starts, coarse_re, coarse_im)
        last_one, (starts, slice_ends) = lax.scan(sweep, start_state, jump_terms)
    return slice_ends
```

```python
import functools

import jax
import jax.numpy as jnp
from jax import lax
from jax.experimental import pallas as pl
from jax.experimental.pallas import tpu as pltpu
from jax.sharding import PartitionSpec as P

FINE = 4
ITERS = 2

step_len = 1.3
half_step = 0.5 * step_len

LANES = 128
SUBLANES = 8
MESH = pl.DeviceIdType.MESH


def members_of(tm, space, columns):
    best = 1
    for count in range(1, tm + 1):
        if tm % count == 0 and columns % (space * count * LANES) == 0:
            best = count
    return best


def kernel(
    sizes, start_ref, depth_ref, coriolis_ref, drag_ref, out_ref,
    state_in, depth_in, coriolis_in, drag_in, stage, recv, coefs, ahead, current, ends, outgoing,
    load_sem, in_send, in_recv, out_send, out_recv,
):
    tm_size, space, members, strip, columns = sizes
    width = columns // (space * members)
    tiles = width // LANES
    lanes = width + LANES
    rows = space * strip
    groups_of_rows = rows // SUBLANES
    peers = space * members
    fields = 6

    time = lax.axis_index("tm")
    place = lax.axis_index("space")
    group = lax.div(time, members)
    member = lax.rem(time, members)
    block = member * space + place

    loads = [
        pltpu.make_async_copy(src, dst, load_sem.at[i])
        for i, (src, dst) in enumerate(
            ((start_ref, state_in), (depth_ref, depth_in), (coriolis_ref, coriolis_in), (drag_ref, drag_in))
        )
    ]
    for load in loads:
        load.start()

    barrier = pltpu.get_barrier_semaphore()
    for away in range(1, peers):
        peer = lax.rem(block + away, peers)
        pl.semaphore_signal(
            barrier, inc=1,
            device_id=(group * members + lax.div(peer, space), lax.rem(peer, space)),
            device_id_type=MESH,
        )
    for load in loads:
        load.wait()

    lane = lax.broadcasted_iota(jnp.int32, (strip, LANES), 1)
    spread = LANES // 4
    for k in range(space):
        base = (member * space + k) * width
        offsets = [base + t * LANES for t in range(tiles)]
        before = lax.rem(base + columns - LANES, columns)
        after = lax.rem(base + width, columns)

        def tile(ref, index, offset):
            window = pl.ds(pl.multiple_of(offset, LANES), LANES)
            return ref[:, window] if index is None else ref[index, :, window]

        def pieces(ref, index=None):
            halo = jnp.where(lane < LANES // 2, tile(ref, index, after), tile(ref, index, before))
            return [tile(ref, index, offset) for offset in offsets] + [halo]

        height, along_x, along_y = [pieces(state_in, f) for f in range(3)]
        height = [half_step * a for a in height]
        depth = [(half_step * half_step) * a for a in pieces(depth_in)]
        angle = [step_len * a for a in pieces(coriolis_in)]
        damping = [jnp.exp(-a) for a in pieces(drag_in)]
        cosine = [d * jnp.cos(a) for d, a in zip(damping, angle)]
        sine = [d * jnp.sin(a) for d, a in zip(damping, angle)]
        everything = (height, along_x, along_y, depth, cosine, sine)
        for f, parts in enumerate(everything):
            for t in range(tiles):
                stage[k, f * tiles + t] = parts[t]
        for first in range(0, fields, 4):
            packed = everything[first][-1]
            for f in range(first + 1, min(first + 4, fields)):
                moved = pltpu.roll(everything[f][-1], spread * (f - first), 1)
                low = spread * (f - first) - spread // 2
                packed = jnp.where((lane >= low) & (lane < low + spread), moved, packed)
            stage[k, fields * tiles + first // 4] = packed

    recv[:, pl.ds(pl.multiple_of(place * strip, strip), strip), :] = stage[place]

    pl.semaphore_wait(barrier, peers - 1)

    def strip_copy(target, source):
        return pltpu.make_async_remote_copy(
            src_ref=stage.at[target],
            dst_ref=recv.at[:, pl.ds(pl.multiple_of(source * strip, strip), strip), :],
            send_sem=in_send.at[target],
            recv_sem=in_recv.at[source],
            device_id=(time, target),
            device_id_type=MESH,
        )

    others = [lax.rem(place + away, space) for away in range(1, space)]
    for k in others:
        strip_copy(k, place).start()
    for k in others:
        strip_copy(k, k).wait_recv()

    def slab(tile_index, j):
        return recv[tile_index, pl.ds(j, SUBLANES, stride=groups_of_rows), :]

    for j in range(groups_of_rows):
        whole = []
        for f in range(fields):
            parts = [slab(f * tiles + t, j) for t in range(tiles)]
            halo = slab(fields * tiles + f // 4, j)
            if f % 4:
                halo = pltpu.roll(halo, LANES - spread * (f % 4), 1)
            whole.append(jnp.concatenate(parts + [halo], axis=1))
        for f in range(3):
            ahead[f, j] = whole[f]
            current[f, j] = whole[f]
            ends[f, j] = whole[f][:, :width]
            coefs[f, j] = whole[3 + f]
        one_re, one_im = whole[4], -whole[5]
        power_re, power_im = one_re, one_im
        for _ in range(FINE - 1):
            power_re, power_im = (
                power_re * one_re - power_im * one_im, power_re * one_im + power_im * one_re
            )
        coefs[3, j] = power_re
        coefs[4, j] = power_im

    def across_rows(a):
        first = pltpu.roll(a[0], SUBLANES - 1, 0)[None]
        last = pltpu.roll(a[-1], 1, 0)[None]
        return jnp.concatenate([a[1:], first], axis=0) - jnp.concatenate([last, a[:-1]], axis=0)

    def across_columns(a):
        return pltpu.roll(a, lanes - 1, 2) - pltpu.roll(a, 1, 2)

    def fine_step(state):
        height, along_x, along_y = state
        depth, cosine, sine = coefs[0], coefs[1], coefs[2]
        height = height - (across_rows(depth * along_x) + across_columns(depth * along_y))
        new_x = cosine * along_x + sine * along_y - across_rows(height)
        new_y = cosine * along_y - sine * along_x - across_columns(height)
        return height, new_x, new_y

    def coarse(state, part):
        height, along_x, along_y = state
        power_re, power_im = coefs[3, :, :, :part], coefs[4, :, :, :part]
        return (
            height,
            power_re * along_x - power_im * along_y,
            power_im * along_x + power_re * along_y,
        )

    def end_copy(local, target, source, t):
        offset = source * width + t * LANES
        return pltpu.make_async_remote_copy(
            src_ref=outgoing.at[local, :, t, pl.ds(pl.multiple_of(target * strip, strip), strip), :],
            dst_ref=out_ref.at[0, :, :, pl.ds(pl.multiple_of(offset, LANES), LANES)],
            send_sem=out_send.at[local, target, t],
            recv_sem=out_recv.at[source, t],
            device_id=(group * members + local, target),
            device_id_type=MESH,
        )

    def one_slice(n, carry):
        a = (ahead[0], ahead[1], ahead[2])
        b = (current[0], current[1], current[2])
        fine_a, fine_b = a, b
        for _ in range(FINE):
            fine_a, fine_b = fine_step(fine_a), fine_step(fine_b)
        coarse_a, coarse_b = coarse(a, lanes), coarse(b, lanes)
        ended = coarse((ends[0], ends[1], ends[2]), width)
        ended = [
            e + (f[:, :, :width] - g[:, :, :width]) for e, f, g in zip(ended, fine_b, coarse_b)
        ]
        for f in range(3):
            current[f] = coarse_b[f] + (fine_a[f] - coarse_a[f])
            ends[f] = ended[f]
        ahead[1] = coarse_a[1]
        ahead[2] = coarse_a[2]

        @pl.when(n >= group * members)
        def _():
            local = n - group * members
            for f in range(3):
                value = ended[f] * (1.0 / half_step) if f == 0 else ended[f]
                for j in range(groups_of_rows):
                    for t in range(tiles):
                        outgoing[local, f, t, pl.ds(j, SUBLANES, stride=groups_of_rows), :] = (
                            value[j, :, t * LANES:(t + 1) * LANES]
                        )
            for away in range(space):
                target = lax.rem(place + away, space)
                if away == 0:
                    @pl.when(local == member)
                    def _():
                        for t in range(tiles):
                            offset = block * width + t * LANES
                            for f in range(3):
                                out_ref[0, f, :, pl.ds(pl.multiple_of(offset, LANES), LANES)] = outgoing[
                                    local, f, t, pl.ds(pl.multiple_of(place * strip, strip), strip), :
                                ]

                    @pl.when(local != member)
                    def _():
                        for t in range(tiles):
                            end_copy(local, target, block, t).start()
                else:
                    for t in range(tiles):
                        end_copy(local, target, block, t).start()

        return carry

    lax.fori_loop(0, (group + 1) * members, one_slice, 0)

    for away in range(1, peers):
        peer = lax.rem(block + away, peers)
        for t in range(tiles):
            end_copy(lax.div(peer, space), lax.rem(peer, space), peer, t).wait_recv()
    for away in range(1, peers):
        peer = lax.rem(block + away, peers)
        for t in range(tiles):
            end_copy(lax.div(peer, space), lax.rem(peer, space), block, t).wait_send()
    for k in others:
        strip_copy(k, place).wait_send()


def on_device(sizes, start_state, still_depth, coriolis, drag_rate):
    tm_size, space, members, strip, columns = sizes
    width = columns // (space * members)
    tiles = width // LANES
    lanes = width + LANES
    rows = space * strip
    slabs = rows // SUBLANES
    peers = space * members
    staged = 6 * tiles + 2
    f32 = jnp.float32
    return pl.pallas_call(
        functools.partial(kernel, sizes),
        out_shape=jax.ShapeDtypeStruct((1, 3, strip, columns), f32),
        in_specs=[pl.BlockSpec(memory_space=pl.ANY)] * 4,
        out_specs=pl.BlockSpec(memory_space=pltpu.VMEM),
        scratch_shapes=[
            pltpu.VMEM((3, strip, columns), f32),
            pltpu.VMEM((strip, columns), f32),
            pltpu.VMEM((strip, columns), f32),
            pltpu.VMEM((strip, columns), f32),
            pltpu.VMEM((space, staged, strip, LANES), f32),
            pltpu.VMEM((staged, rows, LANES), f32),
            pltpu.VMEM((5, slabs, SUBLANES, lanes), f32),
            pltpu.VMEM((3, slabs, SUBLANES, lanes), f32),
            pltpu.VMEM((3, slabs, SUBLANES, lanes), f32),
            pltpu.VMEM((3, slabs, SUBLANES, width), f32),
            pltpu.VMEM((members, 3, tiles, rows, LANES), f32),
            pltpu.SemaphoreType.DMA((4,)),
            pltpu.SemaphoreType.DMA((space,)),
            pltpu.SemaphoreType.DMA((space,)),
            pltpu.SemaphoreType.DMA((members, space, tiles)),
            pltpu.SemaphoreType.DMA((peers, tiles)),
        ],
        compiler_params=pltpu.CompilerParams(collective_id=0, has_side_effects=True),
    )(start_state, still_depth, coriolis, drag_rate)


def solution(mesh):
    tm_size, space = mesh.shape["tm"], mesh.shape["space"]

    def body(start_state, still_depth, coriolis, drag_rate):
        strip, columns = still_depth.shape
        assert 2 * FINE * ITERS <= LANES // 8 and strip % SUBLANES == 0
        members = members_of(tm_size, space, columns)
        sizes = (tm_size, space, members, strip, columns)
        return on_device(sizes, start_state, still_depth, coriolis, drag_rate)

    placed = (P(None, "space", None), P("space", None), P("space", None), P("space", None))
    return jax.shard_map(
        body,
        mesh=mesh,
        in_specs=placed,
        out_specs=P("tm", None, "space", None),
        check_vma=False,
    )
```

```python
import functools

import jax
import jax.numpy as jnp
from jax import lax
from jax.experimental import pallas as pl
from jax.experimental.pallas import tpu as pltpu
from jax.sharding import PartitionSpec as P

FINE = 4
ITERS = 2

step_len = 1.3
half_step = 0.5 * step_len

LANES = 128
SUBLANES = 8
MESH = pl.DeviceIdType.MESH


def members_of(tm, space, columns):
    best = 1
    for count in range(1, tm + 1):
        if tm % count == 0 and columns % (space * count * LANES) == 0:
            best = count
    return best


def kernel(
    sizes, start_ref, depth_ref, coriolis_ref, drag_ref, out_ref,
    state_in, depth_in, coriolis_in, drag_in, stage, recv, coefs, ahead, current, ends, outgoing,
    load_sem, in_send, in_recv, out_send, out_recv,
):
    tm_size, space, members, strip, columns = sizes
    width = columns // (space * members)
    tiles = width // LANES
    lanes = width + LANES
    rows = space * strip
    groups_of_rows = rows // SUBLANES
    peers = space * members
    fields = 6

    time = lax.axis_index("tm")
    place = lax.axis_index("space")
    group = lax.div(time, members)
    member = lax.rem(time, members)
    block = member * space + place

    loads = [
        pltpu.make_async_copy(src, dst, load_sem.at[i])
        for i, (src, dst) in enumerate(
            ((start_ref, state_in), (depth_ref, depth_in), (coriolis_ref, coriolis_in), (drag_ref, drag_in))
        )
    ]
    for load in loads:
        load.start()

    barrier = pltpu.get_barrier_semaphore()
    for away in range(1, peers):
        peer = lax.rem(block + away, peers)
        pl.semaphore_signal(
            barrier, inc=1,
            device_id=(group * members + lax.div(peer, space), lax.rem(peer, space)),
            device_id_type=MESH,
        )
    for load in loads:
        load.wait()

    lane = lax.broadcasted_iota(jnp.int32, (strip, LANES), 1)
    spread = LANES // 4
    for k in range(space):
        base = (member * space + k) * width
        offsets = [base + t * LANES for t in range(tiles)]
        before = lax.rem(base + columns - LANES, columns)
        after = lax.rem(base + width, columns)

        def tile(ref, index, offset):
            window = pl.ds(pl.multiple_of(offset, LANES), LANES)
            return ref[:, window] if index is None else ref[index, :, window]

        def pieces(ref, index=None):
            halo = jnp.where(lane < LANES // 2, tile(ref, index, after), tile(ref, index, before))
            return [tile(ref, index, offset) for offset in offsets] + [halo]

        height, along_x, along_y = [pieces(state_in, f) for f in range(3)]
        height = [half_step * a for a in height]
        depth = [(half_step * half_step) * a for a in pieces(depth_in)]
        angle = [step_len * a for a in pieces(coriolis_in)]
        damping = [jnp.exp(-a) for a in pieces(drag_in)]
        cosine = [d * jnp.cos(a) for d, a in zip(damping, angle)]
        sine = [d * jnp.sin(a) for d, a in zip(damping, angle)]
        everything = (height, along_x, along_y, depth, cosine, sine)
        for f, parts in enumerate(everything):
            for t in range(tiles):
                stage[k, f * tiles + t] = parts[t]
        for first in range(0, fields, 4):
            packed = everything[first][-1]
            for f in range(first + 1, min(first + 4, fields)):
                moved = pltpu.roll(everything[f][-1], spread * (f - first), 1)
                low = spread * (f - first) - spread // 2
                packed = jnp.where((lane >= low) & (lane < low + spread), moved, packed)
            stage[k, fields * tiles + first // 4] = packed

    recv[:, pl.ds(pl.multiple_of(place * strip, strip), strip), :] = stage[place]

    pl.semaphore_wait(barrier, peers - 1)

    def strip_copy(target, source):
        return pltpu.make_async_remote_copy(
            src_ref=stage.at[target],
            dst_ref=recv.at[:, pl.ds(pl.multiple_of(source * strip, strip), strip), :],
            send_sem=in_send.at[target],
            recv_sem=in_recv.at[source],
            device_id=(time, target),
            device_id_type=MESH,
        )

    others = [lax.rem(place + away, space) for away in range(1, space)]
    for k in others:
        strip_copy(k, place).start()
    for k in others:
        strip_copy(k, k).wait_recv()

    def slab(tile_index, j):
        return recv[tile_index, pl.ds(j, SUBLANES, stride=groups_of_rows), :]

    for j in range(groups_of_rows):
        whole = []
        for f in range(fields):
            parts = [slab(f * tiles + t, j) for t in range(tiles)]
            halo = slab(fields * tiles + f // 4, j)
            if f % 4:
                halo = pltpu.roll(halo, LANES - spread * (f % 4), 1)
            whole.append(jnp.concatenate(parts + [halo], axis=1))
        for f in range(3):
            ahead[f, j] = whole[f]
            current[f, j] = whole[f]
            ends[f, j] = whole[f][:, :width]
            coefs[f, j] = whole[3 + f]
        one_re, one_im = whole[4], -whole[5]
        power_re, power_im = one_re, one_im
        for _ in range(FINE - 1):
            power_re, power_im = (
                power_re * one_re - power_im * one_im, power_re * one_im + power_im * one_re
            )
        coefs[3, j] = power_re
        coefs[4, j] = power_im

    def across_rows(a):
        first = pltpu.roll(a[0], SUBLANES - 1, 0)[None]
        last = pltpu.roll(a[-1], 1, 0)[None]
        return jnp.concatenate([a[1:], first], axis=0) - jnp.concatenate([last, a[:-1]], axis=0)

    def across_columns(a):
        return pltpu.roll(a, lanes - 1, 2) - pltpu.roll(a, 1, 2)

    def fine_step(state):
        height, along_x, along_y = state
        depth, cosine, sine = coefs[0], coefs[1], coefs[2]
        height = height - (across_rows(depth * along_x) + across_columns(depth * along_y))
        new_x = cosine * along_x + sine * along_y - across_rows(height)
        new_y = cosine * along_y - sine * along_x - across_columns(height)
        return height, new_x, new_y

    def coarse(state, part):
        height, along_x, along_y = state
        power_re, power_im = coefs[3, :, :, :part], coefs[4, :, :, :part]
        return (
            height,
            power_re * along_x - power_im * along_y,
            power_im * along_x + power_re * along_y,
        )

    def end_copy(local, target, source, t):
        offset = source * width + t * LANES
        return pltpu.make_async_remote_copy(
            src_ref=outgoing.at[local, :, t, pl.ds(pl.multiple_of(target * strip, strip), strip), :],
            dst_ref=out_ref.at[0, :, :, pl.ds(pl.multiple_of(offset, LANES), LANES)],
            send_sem=out_send.at[local, target, t],
            recv_sem=out_recv.at[source, t],
            device_id=(group * members + local, target),
            device_id_type=MESH,
        )

    def one_slice(n, carry):
        a = (ahead[0], ahead[1], ahead[2])
        b = (current[0], current[1], current[2])
        fine_a, fine_b = a, b
        for _ in range(FINE):
            fine_a, fine_b = fine_step(fine_a), fine_step(fine_b)
        coarse_a, coarse_b = coarse(a, lanes), coarse(b, lanes)
        ended = coarse((ends[0], ends[1], ends[2]), width)
        ended = [
            e + (f[:, :, :width] - g[:, :, :width]) for e, f, g in zip(ended, fine_b, coarse_b)
        ]
        for f in range(3):
            current[f] = coarse_b[f] + (fine_a[f] - coarse_a[f])
            ends[f] = ended[f]
        ahead[1] = coarse_a[1]
        ahead[2] = coarse_a[2]

        @pl.when(n >= group * members)
        def _():
            local = n - group * members
            for f in range(3):
                value = ended[f] * (1.0 / half_step) if f == 0 else ended[f]
                for j in range(groups_of_rows):
                    for t in range(tiles):
                        outgoing[local, f, t, pl.ds(j, SUBLANES, stride=groups_of_rows), :] = (
                            value[j, :, t * LANES:(t + 1) * LANES]
                        )
            for away in range(space):
                target = lax.rem(place + away, space)
                if away == 0:
                    @pl.when(local == member)
                    def _():
                        for t in range(tiles):
                            offset = block * width + t * LANES
                            for f in range(3):
                                out_ref[0, f, :, pl.ds(pl.multiple_of(offset, LANES), LANES)] = outgoing[
                                    local, f, t, pl.ds(pl.multiple_of(place * strip, strip), strip), :
                                ]

                    @pl.when(local != member)
                    def _():
                        for t in range(tiles):
                            end_copy(local, target, block, t).start()
                else:
                    for t in range(tiles):
                        end_copy(local, target, block, t).start()

        return carry

    lax.fori_loop(0, (group + 1) * members, one_slice, 0)

    for away in range(1, peers):
        peer = lax.rem(block + away, peers)
        for t in range(tiles):
            end_copy(lax.div(peer, space), lax.rem(peer, space), peer, t).wait_recv()
    for away in range(1, peers):
        peer = lax.rem(block + away, peers)
        for t in range(tiles):
            end_copy(lax.div(peer, space), lax.rem(peer, space), block, t).wait_send()
    for k in others:
        strip_copy(k, place).wait_send()


def on_device(sizes, start_state, still_depth, coriolis, drag_rate):
    tm_size, space, members, strip, columns = sizes
    width = columns // (space * members)
    tiles = width // LANES
    lanes = width + LANES
    rows = space * strip
    slabs = rows // SUBLANES
    peers = space * members
    staged = 6 * tiles + 2
    f32 = jnp.float32
    return pl.pallas_call(
        functools.partial(kernel, sizes),
        out_shape=pltpu.VMEM((1, 3, strip, columns), f32),
        in_specs=[pl.BlockSpec(memory_space=pl.ANY)] * 4,
        out_specs=pl.BlockSpec(memory_space=pltpu.VMEM),
        scratch_shapes=[
            pltpu.VMEM((3, strip, columns), f32),
            pltpu.VMEM((strip, columns), f32),
            pltpu.VMEM((strip, columns), f32),
            pltpu.VMEM((strip, columns), f32),
            pltpu.VMEM((space, staged, strip, LANES), f32),
            pltpu.VMEM((staged, rows, LANES), f32),
            pltpu.VMEM((5, slabs, SUBLANES, lanes), f32),
            pltpu.VMEM((3, slabs, SUBLANES, lanes), f32),
            pltpu.VMEM((3, slabs, SUBLANES, lanes), f32),
            pltpu.VMEM((3, slabs, SUBLANES, width), f32),
            pltpu.VMEM((members, 3, tiles, rows, LANES), f32),
            pltpu.SemaphoreType.DMA((4,)),
            pltpu.SemaphoreType.DMA((space,)),
            pltpu.SemaphoreType.DMA((space,)),
            pltpu.SemaphoreType.DMA((members, space, tiles)),
            pltpu.SemaphoreType.DMA((peers, tiles)),
        ],
        compiler_params=pltpu.CompilerParams(collective_id=0, has_side_effects=True),
    )(start_state, still_depth, coriolis, drag_rate)


def solution(mesh):
    tm_size, space = mesh.shape["tm"], mesh.shape["space"]

    def body(start_state, still_depth, coriolis, drag_rate):
        strip, columns = still_depth.shape
        assert 2 * FINE * ITERS <= LANES // 8 and strip % SUBLANES == 0
        members = members_of(tm_size, space, columns)
        sizes = (tm_size, space, members, strip, columns)
        return on_device(sizes, start_state, still_depth, coriolis, drag_rate)

    placed = (P(None, "space", None), P("space", None), P("space", None), P("space", None))
    return jax.shard_map(
        body,
        mesh=mesh,
        in_specs=placed,
        out_specs=P("tm", None, "space", None),
        check_vma=False,
    )
```

```python
import functools

import jax
import jax.numpy as jnp
from jax import lax
from jax.experimental import pallas as pl
from jax.experimental.pallas import tpu as pltpu
from jax.sharding import PartitionSpec as P

FINE = 4
ITERS = 2

step_len = 1.3
half_step = 0.5 * step_len

LANES = 128
SUBLANES = 8
MESH = pl.DeviceIdType.MESH


def members_of(tm, space, columns):
    best = 1
    for count in range(1, tm + 1):
        if tm % count == 0 and columns % (space * count * LANES) == 0:
            best = count
    return best


def far_first(index, count):
    if count & (count - 1):
        return [lax.rem(index + away, count) for away in range(1, count + 1)]
    return [jnp.bitwise_xor(index, away) for away in range(count - 1, -1, -1)]


def kernel(
    sizes, start_ref, depth_ref, coriolis_ref, drag_ref, out_ref,
    state_in, depth_in, coriolis_in, drag_in, stage, recv, coefs, ahead, current, ends, jumps, outgoing,
    load_sem, in_send, in_recv, out_send, out_recv,
):
    tm_size, space, members, strip, columns = sizes
    width = columns // (space * members)
    tiles = width // LANES
    lanes = width + LANES
    rows = space * strip
    groups_of_rows = rows // SUBLANES
    peers = space * members
    fields = 6

    time = lax.axis_index("tm")
    place = lax.axis_index("space")
    group = lax.div(time, members)
    member = lax.rem(time, members)
    block = member * space + place

    loads = [
        pltpu.make_async_copy(src, dst, load_sem.at[i])
        for i, (src, dst) in enumerate(
            ((start_ref, state_in), (depth_ref, depth_in), (coriolis_ref, coriolis_in), (drag_ref, drag_in))
        )
    ]
    for load in loads:
        load.start()

    barrier = pltpu.get_barrier_semaphore()
    for away in range(1, peers):
        peer = lax.rem(block + away, peers)
        pl.semaphore_signal(
            barrier, inc=1,
            device_id=(group * members + lax.div(peer, space), lax.rem(peer, space)),
            device_id_type=MESH,
        )
    for load in loads:
        load.wait()

    lane = lax.broadcasted_iota(jnp.int32, (strip, LANES), 1)
    spread = LANES // 4
    for k in range(space):
        base = (member * space + k) * width
        offsets = [base + t * LANES for t in range(tiles)]
        before = lax.rem(base + columns - LANES, columns)
        after = lax.rem(base + width, columns)

        def tile(ref, index, offset):
            window = pl.ds(pl.multiple_of(offset, LANES), LANES)
            return ref[:, window] if index is None else ref[index, :, window]

        def pieces(ref, index=None):
            halo = jnp.where(lane < LANES // 2, tile(ref, index, after), tile(ref, index, before))
            return [tile(ref, index, offset) for offset in offsets] + [halo]

        height, along_x, along_y = [pieces(state_in, f) for f in range(3)]
        height = [half_step * a for a in height]
        depth = [(half_step * half_step) * a for a in pieces(depth_in)]
        angle = [step_len * a for a in pieces(coriolis_in)]
        damping = [jnp.exp(-a) for a in pieces(drag_in)]
        cosine = [d * jnp.cos(a) for d, a in zip(damping, angle)]
        sine = [d * jnp.sin(a) for d, a in zip(damping, angle)]
        everything = (height, along_x, along_y, depth, cosine, sine)
        for f, parts in enumerate(everything):
            for t in range(tiles):
                stage[k, f * tiles + t] = parts[t]
        for first in range(0, fields, 4):
            packed = everything[first][-1]
            for f in range(first + 1, min(first + 4, fields)):
                moved = pltpu.roll(everything[f][-1], spread * (f - first), 1)
                low = spread * (f - first) - spread // 2
                packed = jnp.where((lane >= low) & (lane < low + spread), moved, packed)
            stage[k, fields * tiles + first // 4] = packed

    recv[:, pl.ds(pl.multiple_of(place * strip, strip), strip), :] = stage[place]

    pl.semaphore_wait(barrier, peers - 1)

    def strip_copy(target, source):
        return pltpu.make_async_remote_copy(
            src_ref=stage.at[target],
            dst_ref=recv.at[:, pl.ds(pl.multiple_of(source * strip, strip), strip), :],
            send_sem=in_send.at[target],
            recv_sem=in_recv.at[source],
            device_id=(time, target),
            device_id_type=MESH,
        )

    others = far_first(place, space)[:-1]
    for k in others:
        strip_copy(k, place).start()
    for k in others:
        strip_copy(k, k).wait_recv()

    def slab(tile_index, j):
        return recv[tile_index, pl.ds(j, SUBLANES, stride=groups_of_rows), :]

    for j in range(groups_of_rows):
        whole = []
        for f in range(fields):
            parts = [slab(f * tiles + t, j) for t in range(tiles)]
            halo = slab(fields * tiles + f // 4, j)
            if f % 4:
                halo = pltpu.roll(halo, LANES - spread * (f % 4), 1)
            whole.append(jnp.concatenate(parts + [halo], axis=1))
        for f in range(3):
            ahead[f, j] = whole[f]
            current[f, j] = whole[f]
            ends[f, j] = whole[f][:, :width]
            coefs[f, j] = whole[3 + f]
        one_re, one_im = whole[4], -whole[5]
        power_re, power_im = one_re, one_im
        for _ in range(FINE - 1):
            power_re, power_im = (
                power_re * one_re - power_im * one_im, power_re * one_im + power_im * one_re
            )
        coefs[3, j] = power_re
        coefs[4, j] = power_im

    def across_rows(a):
        first = pltpu.roll(a[0], SUBLANES - 1, 0)[None]
        last = pltpu.roll(a[-1], 1, 0)[None]
        return jnp.concatenate([a[1:], first], axis=0) - jnp.concatenate([last, a[:-1]], axis=0)

    def across_columns(a):
        return pltpu.roll(a, lanes - 1, 2) - pltpu.roll(a, 1, 2)

    def fine_step(state):
        height, along_x, along_y = state
        depth, cosine, sine = coefs[0], coefs[1], coefs[2]
        height = height - (across_rows(depth * along_x) + across_columns(depth * along_y))
        new_x = cosine * along_x + sine * along_y - across_rows(height)
        new_y = cosine * along_y - sine * along_x - across_columns(height)
        return height, new_x, new_y

    def coarse(state, part):
        height, along_x, along_y = state
        power_re, power_im = coefs[3, :, :, :part], coefs[4, :, :, :part]
        return (
            height,
            power_re * along_x - power_im * along_y,
            power_im * along_x + power_re * along_y,
        )

    def end_copy(local, target, source, t):
        offset = source * width + t * LANES
        return pltpu.make_async_remote_copy(
            src_ref=outgoing.at[local, :, t, pl.ds(pl.multiple_of(target * strip, strip), strip), :],
            dst_ref=out_ref.at[0, :, :, pl.ds(pl.multiple_of(offset, LANES), LANES)],
            send_sem=out_send.at[local, target, t],
            recv_sem=out_recv.at[source, t],
            device_id=(group * members + local, target),
            device_id_type=MESH,
        )

    def fine(states):
        for _ in range(FINE):
            states = [fine_step(state) for state in states]
        return states

    def first_jumps(batch, carry, count=members):
        state = (ahead[0], ahead[1], ahead[2])
        starts = []
        for _ in range(count):
            starts.append(state)
            state = coarse(state, lanes)
        ahead[1], ahead[2] = state[1], state[2]
        after = starts[1:] + [state]
        for i, (ended, turned) in enumerate(zip(fine(starts), after)):
            for f in range(3):
                jumps[batch * members + i, f] = ended[f] - turned[f]
        return carry

    def last_ends(batch, carry, known=0):
        state = (current[0], current[1], current[2])
        starts, turned = [], []
        for i in range(members):
            starts.append(state)
            turned.append(coarse(state, lanes))
            state = [turned[i][f] + jumps[batch * members + i, f] for f in range(3)]
        for f in range(3):
            current[f] = state[f]
        ended = (ends[0], ends[1], ends[2])
        fine_ends = [None] * known + fine(starts[known:])
        for i, fine_end in enumerate(fine_ends):
            ended = coarse(ended, width)
            if fine_end is None:
                jump = [jumps[i, f, :, :, :width] for f in range(3)]
            else:
                jump = [f[:, :, :width] - g[:, :, :width] for f, g in zip(fine_end, turned[i])]
            ended = [e + a for e, a in zip(ended, jump)]

            @pl.when(batch == group)
            def _():
                put(i, ended)

        for f in range(3):
            ends[f] = ended[f]

        @pl.when(batch == group)
        def _():
            send()

        return carry

    def put(local, ended):
        for f in range(3):
            value = ended[f] * (1.0 / half_step) if f == 0 else ended[f]
            for j in range(groups_of_rows):
                for t in range(tiles):
                    outgoing[local, f, t, pl.ds(j, SUBLANES, stride=groups_of_rows), :] = (
                        value[j, :, t * LANES:(t + 1) * LANES]
                    )

    def send():
        locals_, targets = far_first(member, members), far_first(place, space)
        for a, local in enumerate(locals_):
            for b, target in enumerate(targets):
                if (a, b) != (members - 1, space - 1):
                    for t in range(tiles):
                        end_copy(local, target, block, t).start()
        for t in range(tiles):
            offset = block * width + t * LANES
            for f in range(3):
                out_ref[0, f, :, pl.ds(pl.multiple_of(offset, LANES), LANES)] = outgoing[
                    member, f, t, pl.ds(pl.multiple_of(place * strip, strip), strip), :
                ]

    lax.fori_loop(0, group, first_jumps, 0)
    first_jumps(group, 0, max(members - 1, 1))
    last_ends(0, 0, 1)
    lax.fori_loop(1, group + 1, last_ends, 0)

    for away in range(1, peers):
        peer = lax.rem(block + away, peers)
        for t in range(tiles):
            end_copy(lax.div(peer, space), lax.rem(peer, space), peer, t).wait_recv()
    for away in range(1, peers):
        peer = lax.rem(block + away, peers)
        for t in range(tiles):
            end_copy(lax.div(peer, space), lax.rem(peer, space), block, t).wait_send()
    for k in others:
        strip_copy(k, place).wait_send()


def on_device(sizes, start_state, still_depth, coriolis, drag_rate):
    tm_size, space, members, strip, columns = sizes
    width = columns // (space * members)
    tiles = width // LANES
    lanes = width + LANES
    rows = space * strip
    slabs = rows // SUBLANES
    peers = space * members
    staged = 6 * tiles + 2
    f32 = jnp.float32
    return pl.pallas_call(
        functools.partial(kernel, sizes),
        out_shape=pltpu.VMEM((1, 3, strip, columns), f32),
        in_specs=[pl.BlockSpec(memory_space=pl.ANY)] * 4,
        out_specs=pl.BlockSpec(memory_space=pltpu.VMEM),
        scratch_shapes=[
            pltpu.VMEM((3, strip, columns), f32),
            pltpu.VMEM((strip, columns), f32),
            pltpu.VMEM((strip, columns), f32),
            pltpu.VMEM((strip, columns), f32),
            pltpu.VMEM((space, staged, strip, LANES), f32),
            pltpu.VMEM((staged, rows, LANES), f32),
            pltpu.VMEM((5, slabs, SUBLANES, lanes), f32),
            pltpu.VMEM((3, slabs, SUBLANES, lanes), f32),
            pltpu.VMEM((3, slabs, SUBLANES, lanes), f32),
            pltpu.VMEM((3, slabs, SUBLANES, width), f32),
            pltpu.VMEM((tm_size, 3, slabs, SUBLANES, lanes), f32),
            pltpu.VMEM((members, 3, tiles, rows, LANES), f32),
            pltpu.SemaphoreType.DMA((4,)),
            pltpu.SemaphoreType.DMA((space,)),
            pltpu.SemaphoreType.DMA((space,)),
            pltpu.SemaphoreType.DMA((members, space, tiles)),
            pltpu.SemaphoreType.DMA((peers, tiles)),
        ],
        compiler_params=pltpu.CompilerParams(collective_id=0, has_side_effects=True),
    )(start_state, still_depth, coriolis, drag_rate)


def solution(mesh):
    tm_size, space = mesh.shape["tm"], mesh.shape["space"]

    def body(start_state, still_depth, coriolis, drag_rate):
        strip, columns = still_depth.shape
        assert 2 * FINE * ITERS <= LANES // 8 and strip % SUBLANES == 0
        members = members_of(tm_size, space, columns)
        sizes = (tm_size, space, members, strip, columns)
        return on_device(sizes, start_state, still_depth, coriolis, drag_rate)

    placed = (P(None, "space", None), P("space", None), P("space", None), P("space", None))
    return jax.shard_map(
        body,
        mesh=mesh,
        in_specs=placed,
        out_specs=P("tm", None, "space", None),
        check_vma=False,
    )
```
